512 devices in a mesh: section: 2 (over x_hi), expert: 32 (over z, core), tensor: 8 (over x_lo, y).
Axes of the slice: x: 4 (x_hi: 2, x_lo: 2; x = x_hi * 2 + x_lo), y: 4, z: 16, core: 2. Of those that a mesh axis runs over, the one named last changes fastest.
Arguments:
- tokens: bfloat16 [8192, 2880], P(('section', 'expert'), 'tensor'), may hold values from -6 to 6
- expert_ids: int32 [8192, 4], P(('section', 'expert')), may hold values from 0 to 63, as said below
- gates: float32 [8192, 4], P(('section', 'expert')), may hold values from 0.05 to 0.5
- remap: int32 [64], replicated, may hold values from 0 to 63, as said below
- gate_up: bfloat16 [64, 2, 1440, 2880], P(('section', 'expert'), None, 'tensor'), may hold values from -0.109375 to 0.109375
- down: bfloat16 [64, 1440, 2880], P(('section', 'expert'), None, 'tensor'), may hold values from -0.15625 to 0.15625
- norm_gain: float32 [2880], replicated, may hold values from 0.25 to 1.75
- w_query: bfloat16 [2880, 2048], P(('section', 'expert'), 'tensor'), may hold values from -2 to 2
- w_key: bfloat16 [2880, 512], P(('section', 'expert'), 'tensor'), may hold values from -2 to 2
- w_value: bfloat16 [2880, 512], P(('section', 'expert'), 'tensor'), may hold values from -0.109375 to 0.109375
- w_out: bfloat16 [2048, 2880], P('tensor', ('section', 'expert')), may hold values from -0.125 to 0.125
Outputs:
- stream: bfloat16 [8192, 2880], P(('section', 'expert'), 'tensor')
- attended: bfloat16 [8192, 2880], P(('section', 'expert'), 'tensor')
The draws below stay inside these ranges and needn't reach their ends.
Inputs may be any that keep to these rules, and one draw needn't show every extreme that they name: `remap`: every expert maps to itself, except the 4 experts of one aligned group of 4 (a failed host), which map to 4 different surviving experts. `expert_ids`: each row names 4 different experts, and their images under remap differ too. In every aligned block of 128 rows, after the remap, 4 surviving experts receive exactly 16 picks each, every other surviving expert exactly 8, the experts of the failed host none.
All inputs are finite; a program needn't handle non-finite values.
Results may differ from the reference program's by a relative error of at most 0.033.
Values may be sent and summed in bfloat16 or wider, within the bound.
No kernel may reach another device: no remote copies, remote signals or barrier semaphores. Data moves between devices by JAX's collectives and lax.ppermute only.
A program may use at most 64 MiB of HBM per device.

```python
import math
import jax
import jax.numpy as jnp
from jax import lax

D = 2880
HID = 1440
QH = 32
KVH = 8
HD = 64
TOPK = 4
DOWNED_EXPERTS = 4
TOK_DEV = 128
EXPERT_TOTAL = 64
CAP = 16
SEQ = 4096
TOKENS = 8192


def outage_arrangement(key):
    plan_key = jax.random.fold_in(key, 101)
    key_host, key_pick = jax.random.split(plan_key)
    machine_index = jax.random.randint(key_host, (), 0, EXPERT_TOTAL // DOWNED_EXPERTS)
    entire_expert_list = jnp.arange(EXPERT_TOTAL, dtype=jnp.int32)
    healthy_experts = (entire_expert_list + DOWNED_EXPERTS * (entire_expert_list >= machine_index * DOWNED_EXPERTS).astype(jnp.int32))[:EXPERT_TOTAL - DOWNED_EXPERTS]
    selected_expert = jax.random.permutation(key_pick, EXPERT_TOTAL - DOWNED_EXPERTS)[:DOWNED_EXPERTS]
    adopting_experts = healthy_experts[selected_expert]
    failed = machine_index * DOWNED_EXPERTS + jnp.arange(DOWNED_EXPERTS, dtype=jnp.int32)
    redirect_lookup = entire_expert_list.at[failed].set(adopting_experts)
    backup_expert = entire_expert_list.at[adopting_experts].set(failed)
    return (redirect_lookup, healthy_experts, backup_expert)


def draw_remap(key, part):
    return outage_arrangement(key)[0].astype(jnp.int32)


def draw_expert_ids(key, part):
    redirect_lookup, healthy_experts, backup_expert = outage_arrangement(key)
    block_count = TOKENS // TOK_DEV
    route_key = jax.random.fold_in(key, 202)

    def one_block(block_key):
        key_shuffle_seed, key_shift, key_coin = jax.random.split(block_key, 3)
        ordering_sequence = healthy_experts[jax.random.permutation(key_shuffle_seed, EXPERT_TOTAL - DOWNED_EXPERTS)]
        cycle = jnp.concatenate([ordering_sequence, ordering_sequence[:DOWNED_EXPERTS]])
        shift_by = jax.random.randint(key_shift, (), 0, EXPERT_TOTAL)
        position = (jnp.arange(TOK_DEV * TOPK, dtype=jnp.int32) + shift_by) % EXPERT_TOTAL
        serving = cycle[position]
        coin_flip = jax.random.randint(key_coin, (TOK_DEV * TOPK,), 0, 2)
        logical = jnp.where(coin_flip == 1, backup_expert[serving], serving)
        return logical.reshape(TOK_DEV, TOPK)
    block_ids = jax.vmap(one_block)(jax.random.split(route_key, block_count))
    return block_ids.reshape(TOKENS, TOPK).astype(jnp.int32)


def query_key_pair(key):
    base_key = jax.random.fold_in(key, 303)
    key_query, key_noise = jax.random.split(base_key)
    deviation = math.sqrt(3.0 / D)
    query_weight = jnp.clip(jax.random.normal(key_query, (D, QH * HD), jnp.float32), -6.0, 6.0) * deviation
    noise_weight = jnp.clip(jax.random.normal(key_noise, (D, KVH * HD), jnp.float32), -6.0, 6.0) * deviation
    return (query_weight, noise_weight)


def draw_w_query(key, part):
    query_weight, noise_weight = query_key_pair(key)
    return query_weight.astype(jnp.bfloat16)


def draw_w_key(key, part):
    query_weight, noise_weight = query_key_pair(key)
    return noise_weight.astype(jnp.bfloat16)


def levels(stream_key, extent, cuts, smallest, largest):
    factor_of = 1.0
    for dim, parts in cuts:
        draws = jax.random.uniform(jax.random.fold_in(jax.random.fold_in(stream_key, 6), dim), (parts,), jnp.float32, smallest / len(cuts), largest / len(cuts))
        factor_of = factor_of * jnp.repeat(jnp.exp(draws), extent[dim] // parts).reshape((-1,) + (1,) * (len(extent) - 1 - dim))
    return factor_of


def bell_draw(rng, dims, scale, most, shards=(), kind=jnp.bfloat16):
    values = jax.random.normal(rng, dims, jnp.float32) * scale
    if len(shards) > 0:
        values = levels(rng, dims, shards, -0.22, 0.18) * values
    return jnp.clip(values, min=-most, max=most).astype(kind)


def setup_inputs(seed: int = 0) -> dict:
    key_list = jax.random.split(jax.random.key(seed), 12)
    tokens = bell_draw(key_list[0], (TOKENS, D), 1.0, 6.0, ((0, 64), (1, 8)))
    expert_ids = draw_expert_ids(jax.random.fold_in(key_list[11], 71), 0)
    gates = jnp.clip(jnp.exp(math.log(0.5) - 2.3025851 * jax.random.uniform(key_list[2], (TOKENS, TOPK), jnp.float32) ** levels(key_list[2], (TOKENS, TOPK), ((0, 64),), -0.2, 0.2)), 0.05, 0.5)
    remap = draw_remap(jax.random.fold_in(key_list[11], 71), 0)
    gate_up = bell_draw(key_list[4], (EXPERT_TOTAL, 2, HID, D), D ** -0.5, 0.109375, ((0, 64), (2, 8)))
    down = bell_draw(key_list[5], (EXPERT_TOTAL, HID, D), HID ** -0.5, 0.15625, ((0, 64), (2, 8)))
    norm_gain = jnp.clip(1.0 + 0.15 * jax.random.normal(key_list[6], (D,), jnp.float32), 0.25, 1.75)
    w_query = draw_w_query(jax.random.fold_in(key_list[11], 71), 0)
    w_key = draw_w_key(jax.random.fold_in(key_list[11], 71), 0)
    w_value = bell_draw(key_list[9], (D, KVH * HD), D ** -0.5, 0.109375, ((0, 64), (1, 8)))
    w_out = bell_draw(key_list[10], (QH * HD, D), (QH * HD) ** -0.5, 0.125, ((0, 8), (1, 64)))
    return dict(tokens=tokens, expert_ids=expert_ids, gates=gates, remap=remap, gate_up=gate_up, down=down, norm_gain=norm_gain, w_query=w_query, w_key=w_key, w_value=w_value, w_out=w_out)


def rotate_pairs(values, positions):
    half_size = values.shape[-1] // 2
    freq = jnp.exp(-math.log(150000.0) * jnp.arange(half_size, dtype=jnp.float32) * 2.0 / values.shape[-1])
    angle = positions.astype(jnp.float32)[:, None] * freq[None, :]
    cosine = jnp.cos(angle)[:, None, :]
    sine = jnp.sin(angle)[:, None, :]
    first_half = values[..., :half_size]
    second_half = values[..., half_size:]
    return jnp.concatenate([first_half * cosine - second_half * sine, second_half * cosine + first_half * sine], axis=-1)

def reference(tokens, expert_ids, gates, remap, gate_up, down, norm_gain, w_query, w_key, w_value, w_out):
    physical = remap[expert_ids].reshape(-1).astype(jnp.int32)
    pick_count = physical.shape[0]
    pick_token = (jnp.arange(pick_count, dtype=jnp.int32) // TOPK).astype(jnp.int32)
    limit = TOKENS // TOK_DEV * CAP

    def one_expert(carry, inputs):
        expert_index, weights_in, weights_out = inputs
        selected_expert = physical == expert_index
        order_index = (jnp.cumsum(selected_expert.astype(jnp.int32)) - 1).astype(jnp.int32)
        target = jnp.where(selected_expert, order_index, limit).astype(jnp.int32)
        slot_token = jax.ops.segment_sum(jnp.where(selected_expert, pick_token, 0), target, num_segments=limit + 1)[:limit]
        rows_in = tokens[slot_token.astype(jnp.int32)]
        gate_part = jnp.dot(rows_in, weights_in[0].T, preferred_element_type=jnp.float32)
        up_part = jnp.dot(rows_in, weights_in[1].T, preferred_element_type=jnp.float32)
        hidden = (jax.nn.silu(gate_part) * up_part).astype(jnp.bfloat16)
        result = jnp.dot(hidden, weights_out, preferred_element_type=jnp.float32).astype(jnp.bfloat16)
        taken = result[jnp.clip(order_index, 0, limit - 1).astype(jnp.int32)].astype(jnp.float32)
        return (carry + jnp.where(selected_expert[:, None], taken, jnp.float32(0.0)), None)
    start_carry = jnp.zeros((pick_count, D), jnp.float32)
    per_pick, _ = lax.scan(one_expert, start_carry, (jnp.arange(EXPERT_TOTAL, dtype=jnp.int32), gate_up, down))
    mixture = lax.optimization_barrier(jnp.sum(per_pick.reshape(TOKENS, TOPK, D) * gates[:, :, None].astype(jnp.float32), axis=1))
    stream = (tokens.astype(jnp.float32) + mixture).astype(jnp.bfloat16)
    stream_wide = stream.astype(jnp.float32)
    mean_square = lax.optimization_barrier(jnp.mean(stream_wide * stream_wide, axis=1))
    normed = (stream_wide * lax.rsqrt(mean_square + 1e-05)[:, None] * norm_gain[None, :]).astype(jnp.bfloat16)
    query_raw = jnp.dot(normed, w_query, preferred_element_type=jnp.float32)
    key_raw = jnp.dot(normed, w_key, preferred_element_type=jnp.float32)
    value_raw = jnp.dot(normed, w_value, preferred_element_type=jnp.float32)
    positions = (jnp.arange(TOKENS, dtype=jnp.int32) % SEQ).astype(jnp.int32)
    queries = rotate_pairs(query_raw.reshape(TOKENS, QH, HD), positions).astype(jnp.bfloat16)
    keys = rotate_pairs(key_raw.reshape(TOKENS, KVH, HD), positions).astype(jnp.bfloat16)
    values = value_raw.reshape(TOKENS, KVH, HD).astype(jnp.bfloat16)
    group_size = QH // KVH
    seq_count = TOKENS // SEQ
    query_blocks = queries.reshape(seq_count, SEQ, KVH, group_size, HD).transpose(0, 2, 3, 1, 4).reshape(seq_count * KVH, group_size, SEQ, HD)
    key_blocks = keys.reshape(seq_count, SEQ, KVH, HD).transpose(0, 2, 1, 3).reshape(seq_count * KVH, SEQ, HD)
    value_blocks = values.reshape(seq_count, SEQ, KVH, HD).transpose(0, 2, 1, 3).reshape(seq_count * KVH, SEQ, HD)
    causal = jnp.arange(SEQ)[:, None] >= jnp.arange(SEQ)[None, :]

    def attend(item):
        query_part, key_part, value_part = item
        scores = jnp.einsum('gtd,nd->gtn', query_part.astype(jnp.float32), key_part.astype(jnp.float32), precision=lax.Precision.HIGHEST) / math.sqrt(HD)
        scores = jnp.where(causal[None, :, :], scores, -1e+30)
        top_score = lax.optimization_barrier(jnp.max(scores, axis=-1, keepdims=True))
        weights = jnp.exp(scores - top_score)
        weights = weights / lax.optimization_barrier(jnp.sum(weights, axis=-1, keepdims=True))
        rounded = weights.astype(jnp.bfloat16).astype(jnp.float32)
        return jnp.einsum('gtn,nd->gtd', rounded, value_part.astype(jnp.float32), precision=lax.Precision.HIGHEST)
    head_out = lax.map(attend, (query_blocks, key_blocks, value_blocks))
    heads = head_out.reshape(seq_count, KVH, group_size, SEQ, HD).transpose(0, 3, 1, 2, 4).reshape(TOKENS, QH * HD).astype(jnp.bfloat16)
    attended = jnp.dot(heads, w_out, preferred_element_type=jnp.float32).astype(jnp.bfloat16)
    return (stream, attended)
```

```python
import math

import jax
import jax.numpy as jnp
from jax import lax
from jax.sharding import Mesh
from jax.sharding import PartitionSpec as P

HD = 64
EPSILON = 1e-05
GROUP = ("section", "z", "core")
TENSOR = ("xlo", "y")


def gather_rows(x, axes, count):
    copies = jnp.broadcast_to(x[None], (count,) + x.shape)
    gathered = lax.all_to_all(copies, axes, split_axis=0, concat_axis=0, tiled=True)
    return gathered.reshape((count * x.shape[0],) + x.shape[1:])


def route(expert_ids, gates, remap, groups, capacity):
    token_rows, topk = expert_ids.shape
    experts = jnp.arange(groups, dtype=jnp.int32)
    hit = expert_ids[:, :, None] == experts
    physical = jnp.sum(jnp.where(hit, remap, 0), axis=2)
    picked = physical[:, :, None] == experts
    chosen = jnp.any(picked, axis=1)
    gate = jnp.sum(jnp.where(picked, gates[:, :, None], 0.0), axis=1)
    order = jnp.arange(token_rows, dtype=jnp.int32)
    before = (order[None, :] < order[:, None]).astype(jnp.bfloat16)
    rank = jnp.dot(before, chosen.astype(jnp.bfloat16), preferred_element_type=jnp.float32)
    tag = jnp.where(chosen, rank + 1.0, 0.0).astype(jnp.bfloat16)
    slots = jnp.arange(groups * capacity, dtype=jnp.int32)
    spread = (experts[:, None] == slots[None, :] // capacity).astype(jnp.bfloat16)
    tag_at = jnp.dot(tag, spread, preferred_element_type=jnp.float32)
    here = tag_at == (slots % capacity + 1).astype(jnp.float32)[None, :]
    high = gate.astype(jnp.bfloat16)
    low = (gate - high.astype(jnp.float32)).astype(jnp.bfloat16)
    zero = jnp.zeros((), jnp.bfloat16)
    gate_terms = [
        jnp.where(
            here, jnp.dot(term, spread, preferred_element_type=jnp.float32).astype(jnp.bfloat16), zero
        )
        for term in (high, low)
    ]
    return here.astype(jnp.bfloat16), gate_terms


def rotate(x, cosine, sine):
    a, b = x[:, : HD // 2], x[:, HD // 2 :]
    return jnp.concatenate([a * cosine - b * sine, b * cosine + a * sine], axis=1)


def on_device(
    tokens, expert_ids, gates, remap, gate_up, down, norm_gain, w_query, w_key, w_value, w_out
):
    token_rows, slice_width = tokens.shape
    groups = lax.axis_size(GROUP)
    parts = lax.axis_size(TENSOR)
    width = parts * slice_width
    capacity = 2 * token_rows * expert_ids.shape[1] // groups
    local_hidden = gate_up.shape[2]
    query_width, kv_width = w_query.shape[1], w_key.shape[1]

    weights = lax.all_gather(
        jnp.concatenate([w_query, w_key, w_value, w_out.T], axis=1), GROUP, axis=0, tiled=True
    )

    here, gate_terms = route(expert_ids, gates, remap, groups, capacity)
    outgoing = lax.dot_general(
        here, tokens, (((0,), (0,)), ((), ())), preferred_element_type=jnp.float32
    ).astype(jnp.bfloat16)
    arrived = lax.all_to_all(
        outgoing.reshape(groups, capacity, slice_width), GROUP, split_axis=0, concat_axis=0, tiled=True
    )
    rows_in = gather_rows(arrived.reshape(groups * capacity, slice_width).T, TENSOR, parts)
    projected = jnp.dot(
        gate_up[0].reshape(2 * local_hidden, width), rows_in, preferred_element_type=jnp.float32
    )
    hidden = (jax.nn.silu(projected[:local_hidden]) * projected[local_hidden:]).astype(jnp.bfloat16)
    all_hidden = gather_rows(hidden, TENSOR, parts)
    result = lax.dot_general(
        all_hidden, down[0], (((0,), (0,)), ((), ())), preferred_element_type=jnp.float32
    ).astype(jnp.bfloat16)
    returned = lax.all_to_all(
        result.reshape(groups, capacity, slice_width), GROUP, split_axis=0, concat_axis=0, tiled=True
    ).reshape(groups * capacity, slice_width)
    mixture = sum(
        jnp.dot(term, returned, preferred_element_type=jnp.float32) for term in gate_terms
    )
    stream = (tokens.astype(jnp.float32) + mixture).astype(jnp.bfloat16)

    stream_wide = gather_rows(stream.T, TENSOR, parts).astype(jnp.float32)
    mean_square = jnp.sum(stream_wide * stream_wide, axis=0) / width
    normed = (
        stream_wide * lax.rsqrt(mean_square + EPSILON)[None, :] * norm_gain[:, None]
    ).astype(jnp.bfloat16)
    raw = lax.dot_general(
        weights[:, : query_width + 2 * kv_width],
        normed,
        (((0,), (0,)), ((), ())),
        preferred_element_type=jnp.float32,
    )
    block = lax.axis_index("z") * lax.axis_size("core") + lax.axis_index("core")
    positions = block * token_rows + jnp.arange(token_rows, dtype=jnp.int32)
    freq = jnp.exp(-math.log(150000.0) * jnp.arange(HD // 2, dtype=jnp.float32) * 2.0 / HD)
    angle = freq[:, None] * positions.astype(jnp.float32)[None, :]
    cosine, sine = jnp.cos(angle), jnp.sin(angle)
    heads_here, kv_here = query_width // HD, kv_width // HD
    per_kv = heads_here // kv_here
    queries = rotate(raw[:query_width].reshape(heads_here, HD, token_rows), cosine, sine).astype(
        jnp.bfloat16
    )
    keys = rotate(
        raw[query_width : query_width + kv_width].reshape(kv_here, HD, token_rows), cosine, sine
    ).astype(jnp.bfloat16)
    values = raw[query_width + kv_width :].reshape(kv_here, HD, token_rows).astype(jnp.bfloat16)
    both = jnp.concatenate([keys, values], axis=0).reshape(-1, token_rows)
    every = lax.all_gather(lax.all_gather(both, "z", axis=0), "core", axis=0)
    cores, planes = every.shape[:2]
    every = every.reshape(cores * planes, 2, kv_here, HD, token_rows)
    all_keys, all_values = every[:, 0], every[:, 1]
    grouped = queries.reshape(kv_here, per_kv, HD, token_rows)
    scores = (
        jnp.einsum("kgdt,bkdn->kgtbn", grouped, all_keys, preferred_element_type=jnp.float32)
        / math.sqrt(HD)
    ).reshape(kv_here, per_kv, token_rows, -1)
    key_block = (
        jnp.arange(planes, dtype=jnp.int32)[None, :] * cores
        + jnp.arange(cores, dtype=jnp.int32)[:, None]
    )
    key_positions = (
        key_block.reshape(-1, 1) * token_rows + jnp.arange(token_rows, dtype=jnp.int32)[None, :]
    ).reshape(-1)
    scores = jnp.where(key_positions[None, :] <= positions[:, None], scores, -1e30)
    top = jnp.max(scores, axis=-1, keepdims=True)
    probs = jnp.exp(scores - top)
    total = jnp.sum(probs, axis=-1)
    probs = probs.astype(jnp.bfloat16).reshape(kv_here, per_kv, token_rows, cores * planes, token_rows)
    mixed = jnp.einsum("bkdn,kgtbn->kgdt", all_values, probs, preferred_element_type=jnp.float32)
    heads = (mixed / total[:, :, None, :]).astype(jnp.bfloat16).reshape(query_width, token_rows)

    partial_out = jnp.dot(
        weights[:, query_width + 2 * kv_width :], heads, preferred_element_type=jnp.float32
    ).astype(jnp.bfloat16)
    shares = lax.all_to_all(
        partial_out.reshape(parts, slice_width, token_rows), TENSOR, split_axis=0, concat_axis=0, tiled=True
    )
    attended = jnp.sum(shares.astype(jnp.float32), axis=0).astype(jnp.bfloat16).T
    return (stream, attended)


def solution(mesh):
    planes = mesh.shape["expert"] // 2
    fine = Mesh(
        mesh.devices.reshape(mesh.shape["section"], planes, 2, 2, mesh.shape["tensor"] // 2),
        GROUP + TENSOR,
    )
    return jax.shard_map(
        on_device,
        mesh=fine,
        in_specs=(
            P(GROUP, TENSOR),
            P(GROUP, None),
            P(GROUP, None),
            P(),
            P(GROUP, None, TENSOR, None),
            P(GROUP, None, TENSOR),
            P(),
            P(GROUP, TENSOR),
            P(GROUP, TENSOR),
            P(GROUP, TENSOR),
            P(TENSOR, GROUP),
        ),
        out_specs=(P(GROUP, TENSOR), P(GROUP, TENSOR)),
        check_vma=False,
    )
```

```python
import math

import jax
import jax.numpy as jnp
from jax import lax
from jax.sharding import Mesh
from jax.sharding import PartitionSpec as P

HD = 64
EPSILON = 1e-05
GROUP = ("section", "z", "core")
TENSOR = ("xlo", "y")


def gather_rows(x, axes, count):
    copies = jnp.broadcast_to(x[None], (count,) + x.shape)
    gathered = lax.all_to_all(copies, axes, split_axis=0, concat_axis=0, tiled=True)
    return gathered.reshape((count * x.shape[0],) + x.shape[1:])


def route(expert_ids, gates, remap, groups, capacity):
    token_rows, topk = expert_ids.shape
    experts = jnp.arange(groups, dtype=jnp.int32)
    hit = expert_ids[:, :, None] == experts
    physical = jnp.sum(jnp.where(hit, remap, 0), axis=2)
    picked = physical[:, :, None] == experts
    chosen = jnp.any(picked, axis=1)
    gate = jnp.sum(jnp.where(picked, gates[:, :, None], 0.0), axis=1)
    order = jnp.arange(token_rows, dtype=jnp.int32)
    before = (order[None, :] < order[:, None]).astype(jnp.bfloat16)
    rank = jnp.dot(before, chosen.astype(jnp.bfloat16), preferred_element_type=jnp.float32)
    tag = jnp.where(chosen, rank + 1.0, 0.0).astype(jnp.bfloat16)
    slots = jnp.arange(groups * capacity, dtype=jnp.int32)
    spread = (experts[:, None] == slots[None, :] // capacity).astype(jnp.bfloat16)
    tag_at = jnp.dot(tag, spread, preferred_element_type=jnp.float32)
    here = tag_at == (slots % capacity + 1).astype(jnp.float32)[None, :]
    high = gate.astype(jnp.bfloat16)
    low = (gate - high.astype(jnp.float32)).astype(jnp.bfloat16)
    zero = jnp.zeros((), jnp.bfloat16)
    gate_terms = [
        jnp.where(
            here, jnp.dot(term, spread, preferred_element_type=jnp.float32).astype(jnp.bfloat16), zero
        )
        for term in (high, low)
    ]
    count = jnp.sum(chosen.astype(jnp.float32), axis=0)
    heavy = (count > capacity // 2).astype(jnp.bfloat16)
    return here.astype(jnp.bfloat16), heavy, gate_terms


def rotate(x, cosine, sine):
    a, b = x[:, : HD // 2], x[:, HD // 2 :]
    return jnp.concatenate([a * cosine - b * sine, b * cosine + a * sine], axis=1)


def on_device(
    tokens, expert_ids, gates, remap, gate_up, down, norm_gain, w_query, w_key, w_value, w_out
):
    token_rows, slice_width = tokens.shape
    groups = lax.axis_size(GROUP)
    parts = lax.axis_size(TENSOR)
    width = parts * slice_width
    capacity = 2 * token_rows * expert_ids.shape[1] // groups
    local_hidden = gate_up.shape[2]
    query_width, kv_width = w_query.shape[1], w_key.shape[1]

    share = w_query.shape[0]
    fill = -share % 8
    weights = lax.all_gather(
        jnp.pad(
            jnp.concatenate([w_query, w_key, w_value, w_out.T], axis=1), ((0, fill), (0, 0))
        ),
        GROUP,
        axis=0,
        tiled=True,
    )

    def filled(x):
        return jnp.pad(
            x.reshape(-1, share, x.shape[1]), ((0, 0), (0, fill), (0, 0))
        ).reshape(-1, x.shape[1])

    here, heavy, gate_terms = route(expert_ids, gates, remap, groups, capacity)
    outgoing = lax.dot_general(
        here, tokens, (((0,), (0,)), ((), ())), preferred_element_type=jnp.float32
    ).astype(jnp.bfloat16)
    per_slot = groups // capacity
    flags = jnp.broadcast_to(heavy.reshape(1, capacity, per_slot), (groups, capacity, per_slot))
    outgoing = jnp.concatenate([outgoing.reshape(groups, capacity, slice_width), flags], axis=2)
    arrived = lax.all_to_all(outgoing, GROUP, split_axis=0, concat_axis=0, tiled=True)
    flags = arrived[:, :, slice_width:].astype(jnp.float32)
    arrived = arrived[:, :, :slice_width].reshape(groups * capacity, slice_width)

    half = capacity // 2
    spare = groups * capacity // 8
    me = lax.axis_index(GROUP)
    listed = (
        jnp.arange(capacity, dtype=jnp.int32)[:, None] * per_slot
        + jnp.arange(per_slot, dtype=jnp.int32)[None, :]
    )
    mine = jnp.sum(jnp.where(listed == me, flags, 0.0), axis=(1, 2)).astype(jnp.int32)
    fits = jnp.max(jnp.sum(flags, axis=0)) * half <= spare
    group_order = jnp.arange(groups, dtype=jnp.int32)
    earlier = jnp.sum(jnp.where(group_order[None, :] < group_order[:, None], mine[None, :], 0), axis=1)

    padding = -local_hidden % 8
    into = jnp.pad(gate_up[0], ((0, 0), (0, padding), (0, 0))).reshape(-1, width)
    out_of = jnp.pad(
        down[0].reshape(parts, local_hidden, slice_width), ((0, 0), (0, padding), (0, 0))
    ).reshape(-1, slice_width)

    def expert(columns):
        rows_in = gather_rows(columns, TENSOR, parts)
        projected = jnp.dot(into, rows_in, preferred_element_type=jnp.float32)
        split = local_hidden + padding
        hidden = (jax.nn.silu(projected[:split]) * projected[split:]).astype(jnp.bfloat16)
        return lax.dot_general(
            gather_rows(hidden, TENSOR, parts),
            out_of,
            (((0,), (0,)), ((), ())),
            preferred_element_type=jnp.float32,
        ).astype(jnp.bfloat16)

    def compact(arrived):
        slot = jnp.arange(capacity, dtype=jnp.int32)[None, :]
        extra = groups * half + half * earlier[:, None] + slot - half
        place = jnp.where(
            slot < half,
            half * group_order[:, None] + slot,
            jnp.where(mine[:, None] > 0, extra, -1),
        )
        kept = groups * half + spare
        keep = (
            (place[:, :, None] == jnp.arange(kept, dtype=jnp.int32))
            .astype(jnp.bfloat16)
            .reshape(groups * capacity, kept)
        )
        columns = lax.dot_general(
            arrived, keep, (((0,), (0,)), ((), ())), preferred_element_type=jnp.float32
        ).astype(jnp.bfloat16)
        return jnp.dot(keep, expert(columns), preferred_element_type=jnp.float32).astype(jnp.bfloat16)

    result = lax.cond(fits, compact, lambda arrived: expert(arrived.T), arrived)
    returned = lax.all_to_all(
        result.reshape(groups, capacity, slice_width), GROUP, split_axis=0, concat_axis=0, tiled=True
    ).reshape(groups * capacity, slice_width)
    mixture = sum(
        jnp.dot(term, returned, preferred_element_type=jnp.float32) for term in gate_terms
    )
    stream = (tokens.astype(jnp.float32) + mixture).astype(jnp.bfloat16)

    stream_wide = gather_rows(filled(stream.T), TENSOR, parts).astype(jnp.float32)
    mean_square = jnp.sum(stream_wide * stream_wide, axis=0) / width
    normed = (
        stream_wide * lax.rsqrt(mean_square + EPSILON)[None, :] * filled(norm_gain[:, None])
    ).astype(jnp.bfloat16)
    raw = lax.dot_general(
        weights[:, : query_width + 2 * kv_width],
        normed,
        (((0,), (0,)), ((), ())),
        preferred_element_type=jnp.float32,
    )
    block = lax.axis_index("z") * lax.axis_size("core") + lax.axis_index("core")
    positions = block * token_rows + jnp.arange(token_rows, dtype=jnp.int32)
    freq = jnp.exp(-math.log(150000.0) * jnp.arange(HD // 2, dtype=jnp.float32) * 2.0 / HD)
    angle = freq[:, None] * positions.astype(jnp.float32)[None, :]
    cosine, sine = jnp.cos(angle), jnp.sin(angle)
    heads_here, kv_here = query_width // HD, kv_width // HD
    per_kv = heads_here // kv_here
    queries = rotate(raw[:query_width].reshape(heads_here, HD, token_rows), cosine, sine).astype(
        jnp.bfloat16
    )
    keys = rotate(
        raw[query_width : query_width + kv_width].reshape(kv_here, HD, token_rows), cosine, sine
    ).astype(jnp.bfloat16)
    values = raw[query_width + kv_width :].reshape(kv_here, HD, token_rows).astype(jnp.bfloat16)
    both = jnp.concatenate([keys, values], axis=0).reshape(-1, token_rows)
    own = lax.all_gather(both, "z", axis=0)
    cores, planes = lax.axis_size("core"), own.shape[0]
    other = lax.ppermute(own, "core", [(i, (i + 1) % cores) for i in range(cores)])
    every = jnp.concatenate([own, other], axis=0).reshape(cores * planes, 2, kv_here, HD, token_rows)
    all_keys, all_values = every[:, 0], every[:, 1]
    grouped = queries.reshape(kv_here, per_kv, HD, token_rows)
    scores = (
        jnp.einsum("kgdt,bkdn->kgtbn", grouped, all_keys, preferred_element_type=jnp.float32)
        / math.sqrt(HD)
    ).reshape(kv_here, per_kv, token_rows, -1)
    key_block = (
        jnp.arange(planes, dtype=jnp.int32)[None, :] * cores
        + (jnp.arange(cores, dtype=jnp.int32)[:, None] + lax.axis_index("core")) % cores
    )
    key_positions = (
        key_block.reshape(-1, 1) * token_rows + jnp.arange(token_rows, dtype=jnp.int32)[None, :]
    ).reshape(-1)
    scores = jnp.where(key_positions[None, :] <= positions[:, None], scores, -1e30)
    top = jnp.max(scores, axis=-1, keepdims=True)
    probs = jnp.exp(scores - top)
    total = jnp.sum(probs, axis=-1)
    probs = probs.astype(jnp.bfloat16).reshape(kv_here, per_kv, token_rows, cores * planes, token_rows)
    mixed = jnp.einsum("bkdn,kgtbn->kgdt", all_values, probs, preferred_element_type=jnp.float32)
    heads = (mixed / total[:, :, None, :]).astype(jnp.bfloat16).reshape(query_width, token_rows)

    partial_out = jnp.dot(
        weights[:, query_width + 2 * kv_width :], heads, preferred_element_type=jnp.float32
    ).astype(jnp.bfloat16)
    shares = lax.all_to_all(
        partial_out.reshape(parts, -1, token_rows), TENSOR, split_axis=0, concat_axis=0, tiled=True
    )
    attended = jnp.sum(shares.astype(jnp.float32), axis=0).astype(jnp.bfloat16)
    attended = attended.reshape(-1, share + fill, token_rows)[:, :share]
    attended = attended.reshape(slice_width, token_rows).T
    return (stream, attended)


def solution(mesh):
    planes = mesh.shape["expert"] // 2
    fine = Mesh(
        mesh.devices.reshape(mesh.shape["section"], planes, 2, 2, mesh.shape["tensor"] // 2),
        GROUP + TENSOR,
    )
    return jax.shard_map(
        on_device,
        mesh=fine,
        in_specs=(
            P(GROUP, TENSOR),
            P(GROUP, None),
            P(GROUP, None),
            P(),
            P(GROUP, None, TENSOR, None),
            P(GROUP, None, TENSOR),
            P(),
            P(GROUP, TENSOR),
            P(GROUP, TENSOR),
            P(GROUP, TENSOR),
            P(TENSOR, GROUP),
        ),
        out_specs=(P(GROUP, TENSOR), P(GROUP, TENSOR)),
        check_vma=False,
    )
```

```python
import math

import jax
import jax.numpy as jnp
from jax import lax
from jax.sharding import Mesh
from jax.sharding import PartitionSpec as P

HD = 64
EPSILON = 1e-05
GROUP = ("section", "z", "core")
TENSOR = ("xlo", "y")
SWAP = ((0, 1), (1, 0))


def gather_rows(x, axes, count):
    copies = jnp.broadcast_to(x[None], (count,) + x.shape)
    gathered = lax.all_to_all(copies, axes, split_axis=0, concat_axis=0, tiled=True)
    return gathered.reshape((count * x.shape[0],) + x.shape[1:])


def route(expert_ids, gates, remap, groups, capacity):
    token_rows, topk = expert_ids.shape
    experts = jnp.arange(groups, dtype=jnp.int32)
    hit = expert_ids[:, :, None] == experts
    physical = jnp.sum(jnp.where(hit, remap, 0), axis=2)
    picked = physical[:, :, None] == experts
    chosen = jnp.any(picked, axis=1)
    gate = jnp.sum(jnp.where(picked, gates[:, :, None], 0.0), axis=1)
    order = jnp.arange(token_rows, dtype=jnp.int32)
    before = (order[None, :] < order[:, None]).astype(jnp.bfloat16)
    rank = jnp.dot(before, chosen.astype(jnp.bfloat16), preferred_element_type=jnp.float32)
    tag = jnp.where(chosen, rank + 1.0, 0.0).astype(jnp.bfloat16)
    slots = jnp.arange(groups * capacity, dtype=jnp.int32)
    spread = (experts[:, None] == slots[None, :] // capacity).astype(jnp.bfloat16)
    tag_at = jnp.dot(tag, spread, preferred_element_type=jnp.float32)
    here = tag_at == (slots % capacity + 1).astype(jnp.float32)[None, :]
    high = gate.astype(jnp.bfloat16)
    low = (gate - high.astype(jnp.float32)).astype(jnp.bfloat16)
    zero = jnp.zeros((), jnp.bfloat16)
    gate_terms = [
        jnp.where(
            here, jnp.dot(term, spread, preferred_element_type=jnp.float32).astype(jnp.bfloat16), zero
        )
        for term in (high, low)
    ]
    count = jnp.sum(chosen.astype(jnp.float32), axis=0)
    heavy = (count > capacity // 2).astype(jnp.bfloat16)
    return here.astype(jnp.bfloat16), heavy, gate_terms


def rotate(x, cosine, sine):
    a, b = x[:, : HD // 2], x[:, HD // 2 :]
    return jnp.concatenate([a * cosine - b * sine, b * cosine + a * sine], axis=1)


def on_device(
    tokens, expert_ids, gates, remap, gate_up, down, norm_gain, w_query, w_key, w_value, w_out
):
    token_rows, slice_width = tokens.shape
    groups = lax.axis_size(GROUP)
    parts = lax.axis_size(TENSOR)
    width = parts * slice_width
    capacity = 2 * token_rows * expert_ids.shape[1] // groups
    local_hidden = gate_up.shape[2]
    query_width, kv_width = w_query.shape[1], w_key.shape[1]

    share = w_query.shape[0]
    fill = -share % 8
    cores, planes, sections = lax.axis_size("core"), lax.axis_size("z"), lax.axis_size("section")
    stretch = groups // parts // cores
    second_core = lax.axis_index("core") == 1
    partner_up = lax.ppermute(gate_up, "xlo", SWAP)
    shard = jnp.pad(
        jnp.concatenate([w_query, w_key, w_value, w_out.T], axis=1), ((0, fill), (0, 0))
    )
    across = lax.ppermute(shard, "section", SWAP)
    pair = jnp.where(
        lax.axis_index("section") == 0,
        jnp.concatenate([shard, across], axis=0),
        jnp.concatenate([across, shard], axis=0),
    )

    def own_core_first(x, axis):
        return jnp.where(second_core, jnp.flip(x, axis), x)

    def filled(x):
        x = x.reshape(-1, stretch, cores, share, x.shape[1])
        x = jnp.pad(x, ((0, 0), (0, 0), (0, 0), (0, fill), (0, 0)))
        return own_core_first(x, 2).transpose(0, 2, 1, 3, 4).reshape(-1, x.shape[4])

    here, heavy, gate_terms = route(expert_ids, gates, remap, groups, capacity)
    outgoing = lax.dot_general(
        here, tokens, (((0,), (0,)), ((), ())), preferred_element_type=jnp.float32
    ).astype(jnp.bfloat16)
    per_slot = groups // capacity
    flags = jnp.broadcast_to(heavy.reshape(1, capacity, per_slot), (groups, capacity, per_slot))
    outgoing = jnp.concatenate([outgoing.reshape(groups, capacity, slice_width), flags], axis=2)
    arrived = lax.all_to_all(outgoing, GROUP, split_axis=0, concat_axis=0, tiled=True)
    arrived, pair = lax.optimization_barrier((arrived, pair))
    own_weights = lax.all_gather(pair, "z", axis=0, tiled=True)
    flags = arrived[:, :, slice_width:].astype(jnp.float32)
    arrived = arrived[:, :, :slice_width].reshape(groups * capacity, slice_width)

    halves = lax.axis_size("xlo")
    quarter = capacity // 4
    spare = groups * capacity // 8
    room = groups * quarter + spare
    me = lax.axis_index(GROUP)
    listed = (
        jnp.arange(capacity, dtype=jnp.int32)[:, None] * per_slot
        + jnp.arange(per_slot, dtype=jnp.int32)[None, :]
    )
    mine = jnp.sum(jnp.where(listed == me, flags, 0.0), axis=(1, 2)).astype(jnp.int32)
    fits = jnp.max(jnp.sum(flags, axis=0)) * quarter <= spare
    group_order = jnp.arange(groups, dtype=jnp.int32)
    earlier = jnp.sum(jnp.where(group_order[None, :] < group_order[:, None], mine[None, :], 0), axis=1)

    padding = -local_hidden % 8
    def tiled_units(weight):
        return jnp.pad(weight[0], ((0, 0), (0, padding), (0, 0))).reshape(-1, width)

    into, into_partner = tiled_units(gate_up), tiled_units(partner_up)
    out_of = jnp.pad(
        down[0].reshape(parts, local_hidden, slice_width), ((0, 0), (0, padding), (0, 0))
    )
    crossed = out_of.reshape((halves, parts // halves) + out_of.shape[1:]).transpose(1, 0, 2, 3)
    out_of_half = [
        turned.reshape(-1, slice_width) for turned in (crossed, jnp.flip(crossed, 1))
    ]
    out_of = out_of.reshape(-1, slice_width)

    def hidden_units(weight, rows_in):
        projected = jnp.dot(weight, rows_in, preferred_element_type=jnp.float32)
        split = local_hidden + padding
        return (jax.nn.silu(projected[:split]) * projected[split:]).astype(jnp.bfloat16)

    def put_out(hidden, weight):
        return lax.dot_general(
            hidden, weight, (((0,), (0,)), ((), ())), preferred_element_type=jnp.float32
        ).astype(jnp.bfloat16)

    def whole(arrived):
        rows_in = gather_rows(arrived.T, TENSOR, parts)
        return put_out(gather_rows(hidden_units(into, rows_in), TENSOR, parts), out_of)

    def compact(arrived):
        slot = jnp.arange(capacity, dtype=jnp.int32)[None, :]
        past = slot >= 2 * quarter
        side = slot // quarter % 2
        base = jnp.where(
            past, groups * quarter + quarter * earlier[:, None], quarter * group_order[:, None]
        )
        place = jnp.where(
            jnp.logical_and(past, mine[:, None] == 0), -1, room * side + base + slot % quarter
        )
        keep = (
            (place[:, :, None] == jnp.arange(halves * room, dtype=jnp.int32))
            .astype(jnp.bfloat16)
            .reshape(groups * capacity, halves * room)
        )
        columns = [
            lax.dot_general(
                arrived,
                keep[:, half * room : (half + 1) * room],
                (((0,), (0,)), ((), ())),
                preferred_element_type=jnp.float32,
            ).astype(jnp.bfloat16)
            for half in range(halves)
        ]
        copies = jnp.broadcast_to(
            jnp.stack(columns)[:, None], (halves, parts // halves, slice_width, room)
        )
        rows_in = lax.all_to_all(
            copies.reshape(parts, slice_width, room), TENSOR, split_axis=0, concat_axis=0, tiled=True
        ).reshape(width, room)
        hidden = jnp.concatenate(
            [hidden_units(into, rows_in), hidden_units(into_partner, rows_in)], axis=0
        )
        all_hidden = gather_rows(hidden, TENSOR, parts).reshape(halves, -1, room)
        result = jnp.concatenate(
            [put_out(all_hidden[half], out_of_half[half]) for half in range(halves)], axis=0
        )
        return jnp.dot(keep, result, preferred_element_type=jnp.float32).astype(jnp.bfloat16)

    result = lax.cond(fits, compact, whole, arrived)
    other_weights = lax.ppermute(own_weights, "core", SWAP)
    returned = lax.all_to_all(
        result.reshape(groups, capacity, slice_width), GROUP, split_axis=0, concat_axis=0, tiled=True
    ).reshape(groups * capacity, slice_width)
    mixture = sum(
        jnp.dot(term, returned, preferred_element_type=jnp.float32) for term in gate_terms
    )
    stream = (tokens.astype(jnp.float32) + mixture).astype(jnp.bfloat16)

    stream_wide = gather_rows(filled(stream.T), TENSOR, parts).astype(jnp.float32)
    mean_square = jnp.sum(stream_wide * stream_wide, axis=0) / width
    normed = (
        stream_wide * lax.rsqrt(mean_square + EPSILON)[None, :] * filled(norm_gain[:, None])
    ).astype(jnp.bfloat16)
    normed = normed.reshape(sections, -1, cores, stretch, share + fill, token_rows)
    normed = normed.transpose(2, 1, 3, 0, 4, 5).reshape(cores, -1, token_rows)
    raw = sum(
        lax.dot_general(
            held[:, : query_width + 2 * kv_width],
            normed[which],
            (((0,), (0,)), ((), ())),
            preferred_element_type=jnp.float32,
        )
        for which, held in enumerate((own_weights, other_weights))
    )
    block = lax.axis_index("z") * lax.axis_size("core") + lax.axis_index("core")
    positions = block * token_rows + jnp.arange(token_rows, dtype=jnp.int32)
    freq = jnp.exp(-math.log(150000.0) * jnp.arange(HD // 2, dtype=jnp.float32) * 2.0 / HD)
    angle = freq[:, None] * positions.astype(jnp.float32)[None, :]
    cosine, sine = jnp.cos(angle), jnp.sin(angle)
    heads_here, kv_here = query_width // HD, kv_width // HD
    per_kv = heads_here // kv_here
    queries = rotate(raw[:query_width].reshape(heads_here, HD, token_rows), cosine, sine).astype(
        jnp.bfloat16
    )
    keys = rotate(
        raw[query_width : query_width + kv_width].reshape(kv_here, HD, token_rows), cosine, sine
    ).astype(jnp.bfloat16)
    values = raw[query_width + kv_width :].reshape(kv_here, HD, token_rows).astype(jnp.bfloat16)
    both = jnp.concatenate([keys, values], axis=0).reshape(-1, token_rows)
    own = lax.all_gather(both, "z", axis=0)
    other = lax.ppermute(own, "core", SWAP)
    every = jnp.concatenate([own, other], axis=0).reshape(cores * planes, 2, kv_here, HD, token_rows)
    all_keys, all_values = every[:, 0], every[:, 1]
    grouped = queries.reshape(kv_here, per_kv, HD, token_rows)
    scores = (
        jnp.einsum("kgdt,bkdn->kgtbn", grouped, all_keys, preferred_element_type=jnp.float32)
        / math.sqrt(HD)
    ).reshape(kv_here, per_kv, token_rows, -1)
    key_block = (
        jnp.arange(planes, dtype=jnp.int32)[None, :] * cores
        + (jnp.arange(cores, dtype=jnp.int32)[:, None] + lax.axis_index("core")) % cores
    )
    key_positions = (
        key_block.reshape(-1, 1) * token_rows + jnp.arange(token_rows, dtype=jnp.int32)[None, :]
    ).reshape(-1)
    scores = jnp.where(key_positions[None, :] <= positions[:, None], scores, -1e30)
    top = jnp.max(scores, axis=-1, keepdims=True)
    probs = jnp.exp(scores - top)
    total = jnp.sum(probs, axis=-1)
    probs = probs.astype(jnp.bfloat16).reshape(kv_here, per_kv, token_rows, cores * planes, token_rows)
    mixed = jnp.einsum("bkdn,kgtbn->kgdt", all_values, probs, preferred_element_type=jnp.float32)
    heads = (mixed / total[:, :, None, :]).astype(jnp.bfloat16).reshape(query_width, token_rows)

    partial_out = jnp.stack(
        [
            jnp.dot(
                held[:, query_width + 2 * kv_width :], heads, preferred_element_type=jnp.float32
            ).astype(jnp.bfloat16)
            for held in (own_weights, other_weights)
        ]
    ).reshape(cores, -1, stretch, sections, share + fill, token_rows)
    shares = lax.all_to_all(
        partial_out.transpose(3, 1, 0, 2, 4, 5).reshape(parts, -1, token_rows),
        TENSOR,
        split_axis=0,
        concat_axis=0,
        tiled=True,
    )
    attended = jnp.sum(shares.astype(jnp.float32), axis=0).astype(jnp.bfloat16)
    attended = attended.reshape(cores, stretch, share + fill, token_rows)[:, :, :share]
    attended = own_core_first(attended, 0).transpose(1, 0, 2, 3).reshape(slice_width, token_rows).T
    return (stream, attended)


def solution(mesh):
    planes = mesh.shape["expert"] // 2
    fine = Mesh(
        mesh.devices.reshape(mesh.shape["section"], planes, 2, 2, mesh.shape["tensor"] // 2),
        GROUP + TENSOR,
    )
    return jax.shard_map(
        on_device,
        mesh=fine,
        in_specs=(
            P(GROUP, TENSOR),
            P(GROUP, None),
            P(GROUP, None),
            P(),
            P(GROUP, None, TENSOR, None),
            P(GROUP, None, TENSOR),
            P(),
            P(GROUP, TENSOR),
            P(GROUP, TENSOR),
            P(GROUP, TENSOR),
            P(TENSOR, GROUP),
        ),
        out_specs=(P(GROUP, TENSOR), P(GROUP, TENSOR)),
        check_vma=False,
    )
```
